32 devices in a mesh: ctx: 8 (over z, x), tp: 4 (over y, core).
Axes of the slice: x: 2, y: 2, z: 4, core: 2. Of those that a mesh axis runs over, the one named last changes fastest.
Arguments:
- mel_frames: bfloat16 [65536, 128], P(('ctx', 'tp')), may hold values from -6 to 6
- utterance_ids: int32 [32, 256], P(('ctx', 'tp')), may hold values from 0 to 15, never falling along the last dimension, each value on 1 to 128 neighbouring positions
- frame_counts: int32 [32, 8], replicated, may hold values from 16 to 48, as said below
- input_proj: bfloat16 [128, 256], replicated, may hold values from -0.75 to 0.75
- sub_depthwise: bfloat16 [3, 2, 256], replicated, may hold values from -4 to 4
- sub_pointwise: bfloat16 [3, 256, 256], replicated, may hold values from -0.5 to 0.5
- output_proj: bfloat16 [256, 1024], replicated, may hold values from -0.375 to 0.375
- norm_gain: bfloat16 [1024], replicated, may hold values from 0.099609375 to 1.8984375
- pointwise_one: bfloat16 [1024, 2048], replicated, may hold values from -0.1875 to 0.1875
- depthwise_taps: bfloat16 [9, 1024], replicated, may hold values from -3.5 to 3.5
- pointwise_two: bfloat16 [1024, 1024], replicated, may hold values from -0.1875 to 0.1875
- projector: bfloat16 [1024, 2048], P('tp'), may hold values from -0.1875 to 0.1875
- embed_grads: bfloat16 [8192, 2048], P(('ctx', 'tp')), may hold values from -0.15625 to 0.15625
Outputs:
- llm_embed: bfloat16 [8192, 2048], P(('ctx', 'tp'))
- projector_grad: float32 [1024, 2048], P('tp', 'ctx')
- pointwise_one_grad: float32 [1024, 2048], P(None, ('ctx', 'tp'))
- pointwise_two_grad: float32 [1024, 1024], P(None, ('ctx', 'tp'))
The draws below stay inside these ranges and needn't reach their ends.
Inputs may be any that keep to these rules, and one draw needn't show every extreme that they name: frame_counts[d, c] is 32 plus or minus 256 / 16; the sign is a sign of pack d times a sign of shard c, and each kind of sign is positive for exactly half of the packs or shards. So every row sums to 256, every column to 1024, and the largest count is 48.
All inputs are finite; a program needn't handle non-finite values.
Results may differ from the reference program's by a relative error of at most 0.028.
Values may be sent and summed in bfloat16 or wider, within the bound.
A program may use at most 128 MiB of HBM per device.

```python
import math
import jax
import jax.numpy as jnp
import numpy as np
from jax import lax

MEL = 128
C_SUB = 256
D = 1024
KERNEL = 9
D_LLM = 2048
E = 256
S_CTX = 1024
N_CTX = 8
N_TP = 4
DEVICES = 32


def draw_frame_counts(key, part):
    key_device, key_shard = jax.random.split(jax.random.fold_in(key, 11))
    device_rank = jax.random.permutation(key_device, DEVICES)
    shard_rank = jax.random.permutation(key_shard, N_CTX)
    device_sign = jnp.where(device_rank < DEVICES // 2, 1, -1).astype(jnp.int32)
    shard_sign = jnp.where(shard_rank < N_CTX // 2, 1, -1).astype(jnp.int32)
    return (E // N_CTX + E // (2 * N_CTX) * device_sign[:, None] * shard_sign[None, :]).astype(jnp.int32)


def levels(own_key, shape, shards, least, largest):
    factor_of = 1.0
    for dim, blocks in shards:
        heights = jax.random.uniform(jax.random.fold_in(jax.random.fold_in(own_key, 6), dim), (blocks,), jnp.float32, least / len(shards), largest / len(shards))
        factor_of = factor_of * jnp.repeat(jnp.exp(heights), shape[dim] // blocks).reshape((-1,) + (1,) * (len(shape) - 1 - dim))
    return factor_of


def length_profile(amount, total, limit, lean):
    loads = [(1 << 20) // math.isqrt(grade ** lean) + 1 for grade in range(2, amount + 1)]
    rest, counts = total - limit - (amount - 1), [1] * (amount - 1)
    while rest > 0:
        movable = [i for i in range(amount - 1) if counts[i] < limit]
        whole, budget = sum([loads[i] for i in movable]), rest
        for i in movable:
            addition = min(limit - counts[i], max(1, budget * loads[i] // whole), rest)
            counts[i] = counts[i] + addition
            rest = rest - addition
    return np.array([limit] + counts)


def ragged(stream_key, count, total, reach, lean):
    if count == 2:
        one = jax.random.randint(stream_key, (), max(1, total - reach), min(reach, total - 1) + 1)
        return jnp.stack([one, total - one])
    lengths = jnp.asarray(length_profile(count, total, reach, lean), jnp.int32)
    couples = (count - 1) // 2
    giver, receiver = lengths[1:1 + 2 * couples:2], lengths[2:2 + 2 * couples:2]
    room = jnp.minimum(giver - 1, reach - receiver)
    moved = jax.random.randint(jax.random.fold_in(stream_key, 1), (couples,), 0, 1 << 20) % (room + 1)
    lengths = lengths.at[1:1 + 2 * couples:2].set(giver - moved).at[2:2 + 2 * couples:2].set(receiver + moved)
    return lengths[jax.random.permutation(jax.random.fold_in(stream_key, 2), count)]


def noise(key, extent, scale, most, cuts=(), held_as=jnp.bfloat16):
    level = levels(key, extent, cuts, -0.22, 0.18) if cuts else 1.0
    result = jax.random.normal(key, extent, jnp.float32) * scale * level
    return jnp.minimum(jnp.maximum(result, -most), most).astype(held_as)


def setup_inputs(seed: int = 0) -> dict:
    seeds = jax.random.split(jax.random.key(seed), 14)
    mel_frames = noise(seeds[0], (DEVICES * 8 * E, MEL), 1.0, 6.0, ((0, 32),))
    utterance_ids = jax.vmap(lambda own: jnp.searchsorted(jnp.cumsum(ragged(own, max(4, E // 16), E, E // 2, 2)), jnp.arange(E), side="right"))(jax.random.split(seeds[1], DEVICES)).reshape((DEVICES, E)).astype(jnp.int32)
    frame_counts = draw_frame_counts(jax.random.fold_in(seeds[13], 71), 0)
    input_proj = noise(seeds[3], (MEL, C_SUB), (MEL // 2) ** -0.5, 0.75)
    sub_depthwise = noise(seeds[4], (3, 2, C_SUB), 2 ** -0.5, 4.0)
    sub_pointwise = noise(seeds[5], (3, C_SUB, C_SUB), (C_SUB // 2) ** -0.5, 0.5)
    output_proj = noise(seeds[6], (C_SUB, D), C_SUB ** -0.5, 0.375)
    norm_gain = jnp.clip(1.0 + 0.18 * jax.random.normal(seeds[7], (D,), jnp.float32), 0.099609375, 1.8984375).astype(jnp.bfloat16)
    pointwise_one = noise(seeds[8], (D, 2 * D), D ** -0.5, 0.1875)
    depthwise_taps = noise(seeds[9], (KERNEL, D), 3 ** -0.5, 3.5)
    pointwise_two = noise(seeds[10], (D, D), D ** -0.5, 0.1875)
    projector = noise(seeds[11], (D, D_LLM), D ** -0.5, 0.1875, ((0, 4),))
    embed_grads = noise(seeds[12], (N_CTX * S_CTX, D_LLM), ((N_CTX * S_CTX) ** -0.5), 0.15625, ((0, 32),))
    return dict(mel_frames=mel_frames, utterance_ids=utterance_ids, frame_counts=frame_counts, input_proj=input_proj, sub_depthwise=sub_depthwise, sub_pointwise=sub_pointwise, output_proj=output_proj, norm_gain=norm_gain, pointwise_one=pointwise_one, depthwise_taps=depthwise_taps, pointwise_two=pointwise_two, projector=projector, embed_grads=embed_grads)


def subsample(frames_in, input_proj, sub_depthwise, sub_pointwise, output_proj):
    encoded_rows = frames_in.shape[0] // 8
    channels = input_proj.shape[1]
    hidden = jax.nn.relu(jnp.dot(frames_in, input_proj, preferred_element_type=jnp.float32)).astype(jnp.bfloat16)
    length = 8
    for section_index in range(3):
        grouped = hidden.reshape(encoded_rows, length // 2, 2, channels).astype(jnp.float32)
        tap_pair = sub_depthwise[section_index].astype(jnp.float32)
        strided = (grouped[:, :, 0] * tap_pair[0] + grouped[:, :, 1] * tap_pair[1]).astype(jnp.bfloat16)
        length = length // 2
        hidden = jax.nn.relu(jnp.dot(strided.reshape(encoded_rows * length, channels), sub_pointwise[section_index], preferred_element_type=jnp.float32)).astype(jnp.bfloat16)
    return jnp.dot(hidden, output_proj, preferred_element_type=jnp.float32)

def depthwise(values, segments, kernel):
    row_total = values.shape[0]
    padded = jnp.pad(values, ((4, 4), (0, 0)))
    padded_ids = jnp.pad(segments, 4, constant_values=-1)
    running_sum = jnp.zeros(values.shape, jnp.float32)
    for tap_index in range(9):
        same_utt = (padded_ids[tap_index:tap_index + row_total] == segments).astype(jnp.float32)[:, None]
        running_sum = running_sum + kernel[tap_index] * padded[tap_index:tap_index + row_total] * same_utt
    return running_sum

def depthwise_back(grad_rows, segments, kernel):
    row_total = grad_rows.shape[0]
    padded_ids = jnp.pad(segments, 4, constant_values=-1)
    running_sum = jnp.zeros(grad_rows.shape, jnp.float32)
    for tap_index in range(9):
        same_utt = (padded_ids[tap_index:tap_index + row_total] == segments).astype(jnp.float32)[:, None]
        moved_rows = jnp.pad(grad_rows * same_utt, ((4, 4), (0, 0)))
        running_sum = running_sum + kernel[tap_index] * moved_rows[8 - tap_index:8 - tap_index + row_total]
    return running_sum

def conv_forward(inputs, segments, norm_gain, pointwise_one, depthwise_taps, pointwise_two):
    center = lax.optimization_barrier(jnp.mean(inputs, axis=1, keepdims=True))
    spread = lax.optimization_barrier(jnp.mean(jnp.square(inputs - center), axis=1, keepdims=True))
    normed = ((inputs - center) * lax.rsqrt(spread + 1e-05) * norm_gain.astype(jnp.float32)).astype(jnp.bfloat16)
    raised = jnp.dot(normed, pointwise_one, preferred_element_type=jnp.float32)
    model_width = inputs.shape[1]
    gated_rows = raised[:, :model_width] * jax.nn.sigmoid(raised[:, model_width:])
    mixed_rows = depthwise(gated_rows, segments, depthwise_taps.astype(jnp.float32))
    activated = (mixed_rows * jax.nn.sigmoid(mixed_rows)).astype(jnp.bfloat16)
    output = (inputs + jnp.dot(activated, pointwise_two, preferred_element_type=jnp.float32)).astype(jnp.bfloat16)
    return (output, (normed, raised, mixed_rows, activated))

def conv_backward(output_grad, segments, depthwise_taps, pointwise_two, kept_state):
    normed, raised, mixed_rows, activated = kept_state
    model_width = output_grad.shape[1]
    two_grad = lax.dot_general(activated, output_grad, (((0,), (0,)), ((), ())), preferred_element_type=jnp.float32)
    act_grad = lax.dot_general(output_grad, pointwise_two, (((1,), (1,)), ((), ())), preferred_element_type=jnp.float32)
    sigmoid_mix = jax.nn.sigmoid(mixed_rows)
    mixed_grad = act_grad * (sigmoid_mix + mixed_rows * sigmoid_mix * (1.0 - sigmoid_mix))
    gated_grad = depthwise_back(mixed_grad, segments, depthwise_taps.astype(jnp.float32))
    sigmoid_gate = jax.nn.sigmoid(raised[:, model_width:])
    raised_grad = jnp.concatenate([gated_grad * sigmoid_gate, gated_grad * raised[:, :model_width] * sigmoid_gate * (1.0 - sigmoid_gate)], axis=1).astype(jnp.bfloat16)
    one_grad = lax.dot_general(normed, raised_grad, (((0,), (0,)), ((), ())), preferred_element_type=jnp.float32)
    return (one_grad, two_grad)

def reference(mel_frames, utterance_ids, frame_counts, input_proj, sub_depthwise, sub_pointwise, output_proj, norm_gain, pointwise_one, depthwise_taps, pointwise_two, projector, embed_grads):
    mel_blocks = mel_frames.reshape(DEVICES, 8 * E, MEL)

    def encode(block_pair):
        mel_block, segments = block_pair
        inputs = subsample(mel_block, input_proj, sub_depthwise, sub_pointwise, output_proj)
        output, _ = conv_forward(inputs, segments, norm_gain, pointwise_one, depthwise_taps, pointwise_two)
        return output
    encoded = lax.map(encode, (mel_blocks, utterance_ids))
    row_starts = (jnp.cumsum(frame_counts, axis=1) - frame_counts).astype(jnp.int32)
    shard_starts = (jnp.cumsum(frame_counts, axis=0) - frame_counts).astype(jnp.int32)
    shard_ends = (shard_starts + frame_counts).astype(jnp.int32)
    position = jnp.arange(S_CTX, dtype=jnp.int32)
    source = lax.optimization_barrier(jnp.sum((position[None, :, None] >= shard_ends.T[:, None, :]).astype(jnp.int32), axis=2)).astype(jnp.int32)
    shard_index = jnp.arange(N_CTX, dtype=jnp.int32)[:, None]
    flat_rows = (source * E + row_starts[source, shard_index] + position[None, :] - shard_starts[source, shard_index]).astype(jnp.int32)
    frames = encoded.reshape(DEVICES * E, D)[flat_rows]
    proj_blocks = projector.reshape(N_TP, D // N_TP, D_LLM)

    def embed_shard(shard_frames):
        pieces = shard_frames.reshape(S_CTX, N_TP, D // N_TP)
        running_sum = jnp.zeros((S_CTX, D_LLM), jnp.float32)
        for tp_index in range(N_TP):
            partial_term = jnp.dot(pieces[:, tp_index], proj_blocks[tp_index], preferred_element_type=jnp.float32).astype(jnp.bfloat16)
            running_sum = running_sum + partial_term.astype(jnp.float32)
        return running_sum.astype(jnp.bfloat16)
    llm_embed = lax.map(embed_shard, frames).reshape(N_CTX * S_CTX, D_LLM)
    cotangent = embed_grads.reshape(N_CTX, S_CTX, D_LLM)

    def back_shard(shard_grads):
        return lax.dot_general(shard_grads, projector, (((1,), (1,)), ((), ())), preferred_element_type=jnp.float32).astype(jnp.bfloat16)
    frame_back = lax.map(back_shard, cotangent)

    def accumulate(running, shard_pair):
        shard_frames, shard_grads = shard_pair
        return (running + lax.dot_general(shard_frames, shard_grads, (((0,), (0,)), ((), ())), preferred_element_type=jnp.float32), None)
    projector_grad, _ = lax.scan(accumulate, jnp.zeros((D, D_LLM), jnp.float32), (frames, cotangent))
    row_ends = (row_starts + frame_counts).astype(jnp.int32)
    local_rows = jnp.arange(E, dtype=jnp.int32)
    target = lax.optimization_barrier(jnp.sum((local_rows[None, :, None] >= row_ends[:, None, :]).astype(jnp.int32), axis=2)).astype(jnp.int32)
    device_index = jnp.arange(DEVICES, dtype=jnp.int32)[:, None]
    back_rows = (target * S_CTX + shard_starts[device_index, target] + local_rows[None, :] - row_starts[device_index, target]).astype(jnp.int32)
    encoded_grads = frame_back.reshape(N_CTX * S_CTX, D)[back_rows]

    def backward_step(running, block_triple):
        mel_block, segments, output_grad = block_triple
        inputs = subsample(mel_block, input_proj, sub_depthwise, sub_pointwise, output_proj)
        _, kept_state = conv_forward(inputs, segments, norm_gain, pointwise_one, depthwise_taps, pointwise_two)
        one_grad, two_grad = conv_backward(output_grad, segments, depthwise_taps, pointwise_two, kept_state)
        return ((running[0] + one_grad, running[1] + two_grad), None)
    start_sums = (jnp.zeros((D, 2 * D), jnp.float32), jnp.zeros((D, D), jnp.float32))
    (one_total, two_total), _ = lax.scan(backward_step, start_sums, (mel_blocks, utterance_ids, encoded_grads))
    return (llm_embed, projector_grad, one_total, two_total)
```

```python
import jax
import jax.numpy as jnp
from jax import lax
from jax.sharding import PartitionSpec as P


def exchange(value, axis_name, flip):
    size = lax.axis_size(axis_name)
    return lax.ppermute(value, axis_name, [(rank, rank ^ flip) for rank in range(size)])


def axis_bits(axis_name):
    return lax.axis_size(axis_name).bit_length() - 1


def gather_blocks(block, axis_name):
    blocks = {0: block}
    for bit in reversed(range(axis_bits(axis_name))):
        for flip, held in list(blocks.items()):
            blocks[flip ^ (1 << bit)] = exchange(held, axis_name, 1 << bit)
    return [blocks[flip] for flip in range(lax.axis_size(axis_name))]


def fold_scatter(value, order):
    layout = sorted(order, key=lambda step: (step[0] != "ctx", -step[1]))
    for position, step in enumerate(order):
        axis_name, bit = step
        dim = layout.index(step)
        layout.remove(step)
        mine = (lax.axis_index(axis_name) >> bit) & 1
        keep = lax.dynamic_index_in_dim(value, mine, dim, keepdims=False)
        send = lax.dynamic_index_in_dim(value, 1 - mine, dim, keepdims=False)
        came = exchange(send, axis_name, 1 << bit)
        value = keep.astype(jnp.float32) + came.astype(jnp.float32)
        if position + 1 < len(order):
            value = value.astype(jnp.bfloat16)
    return value


def split_bits(value, steps):
    return value.reshape((2,) * steps + (value.shape[0] >> steps,) + value.shape[1:])


def subsample(frames_in, input_proj, sub_depthwise, sub_pointwise, output_proj):
    encoded_rows = frames_in.shape[0] // 8
    channels = input_proj.shape[1]
    by_phase = frames_in.reshape(encoded_rows, 8, frames_in.shape[1]).transpose(1, 0, 2)
    hidden = jax.nn.relu(
        jnp.dot(
            by_phase.reshape(8 * encoded_rows, frames_in.shape[1]),
            input_proj,
            preferred_element_type=jnp.float32,
        )
    ).astype(jnp.bfloat16)
    length = 8
    for section_index in range(3):
        length = length // 2
        grouped = hidden.reshape(length, 2, encoded_rows, channels).astype(jnp.float32)
        tap_pair = sub_depthwise[section_index].astype(jnp.float32)
        strided = (grouped[:, 0] * tap_pair[0] + grouped[:, 1] * tap_pair[1]).astype(jnp.bfloat16)
        hidden = jax.nn.relu(
            jnp.dot(
                strided.reshape(length * encoded_rows, channels),
                sub_pointwise[section_index],
                preferred_element_type=jnp.float32,
            )
        ).astype(jnp.bfloat16)
    return jnp.dot(hidden, output_proj, preferred_element_type=jnp.float32)


def depthwise(values, segments, kernel):
    row_total = values.shape[0]
    padded = jnp.pad(values, ((4, 4), (0, 0)))
    padded_ids = jnp.pad(segments, 4, constant_values=-1)
    running_sum = jnp.zeros(values.shape, jnp.float32)
    for tap_index in range(9):
        same_utt = (padded_ids[tap_index : tap_index + row_total] == segments).astype(jnp.float32)[
            :, None
        ]
        running_sum = (
            running_sum + kernel[tap_index] * padded[tap_index : tap_index + row_total] * same_utt
        )
    return running_sum


def depthwise_back(grad_rows, segments, kernel):
    row_total = grad_rows.shape[0]
    padded_ids = jnp.pad(segments, 4, constant_values=-1)
    running_sum = jnp.zeros(grad_rows.shape, jnp.float32)
    for tap_index in range(9):
        same_utt = (padded_ids[tap_index : tap_index + row_total] == segments).astype(jnp.float32)[
            :, None
        ]
        moved_rows = jnp.pad(grad_rows * same_utt, ((4, 4), (0, 0)))
        running_sum = (
            running_sum + kernel[tap_index] * moved_rows[8 - tap_index : 8 - tap_index + row_total]
        )
    return running_sum


def conv_forward(inputs, segments, norm_gain, pointwise_one, depthwise_taps, pointwise_two):
    center = jnp.mean(inputs, axis=1, keepdims=True)
    spread = jnp.mean(jnp.square(inputs - center), axis=1, keepdims=True)
    normed = ((inputs - center) * lax.rsqrt(spread + 1e-05) * norm_gain.astype(jnp.float32)).astype(
        jnp.bfloat16
    )
    raised = jnp.dot(normed, pointwise_one, preferred_element_type=jnp.float32)
    model_width = inputs.shape[1]
    gated_rows = raised[:, :model_width] * jax.nn.sigmoid(raised[:, model_width:])
    mixed_rows = depthwise(gated_rows, segments, depthwise_taps.astype(jnp.float32))
    activated = (mixed_rows * jax.nn.sigmoid(mixed_rows)).astype(jnp.bfloat16)
    output = (
        inputs + jnp.dot(activated, pointwise_two, preferred_element_type=jnp.float32)
    ).astype(jnp.bfloat16)
    return (output, (normed, raised, mixed_rows, activated))


def raised_backward(output_grad, segments, depthwise_taps, pointwise_two, kept_state):
    normed, raised, mixed_rows, activated = kept_state
    model_width = output_grad.shape[1]
    act_grad = lax.dot_general(
        output_grad, pointwise_two, (((1,), (1,)), ((), ())), preferred_element_type=jnp.float32
    )
    sigmoid_mix = jax.nn.sigmoid(mixed_rows)
    mixed_grad = act_grad * (sigmoid_mix + mixed_rows * sigmoid_mix * (1.0 - sigmoid_mix))
    gated_grad = depthwise_back(mixed_grad, segments, depthwise_taps.astype(jnp.float32))
    sigmoid_gate = jax.nn.sigmoid(raised[:, model_width:])
    return jnp.concatenate(
        [
            gated_grad * sigmoid_gate,
            gated_grad * raised[:, :model_width] * sigmoid_gate * (1.0 - sigmoid_gate),
        ],
        axis=1,
    ).astype(jnp.bfloat16)


def rows_product(left, right):
    return lax.dot_general(
        left, right, (((0,), (0,)), ((), ())), preferred_element_type=jnp.float32
    )


def pick(wanted, slots, rows):
    chosen = (wanted[:, None] == slots[None, :]).astype(jnp.bfloat16)
    return jnp.dot(chosen, rows, preferred_element_type=jnp.float32).astype(jnp.bfloat16)


def body(
    mel_frames,
    utterance_ids,
    frame_counts,
    input_proj,
    sub_depthwise,
    sub_pointwise,
    output_proj,
    norm_gain,
    pointwise_one,
    depthwise_taps,
    pointwise_two,
    projector,
    embed_grads,
):
    ctx_count = lax.axis_size("ctx")
    tp_count = lax.axis_size("tp")
    device_count = ctx_count * tp_count
    ctx_rank = lax.axis_index("ctx")
    tp_rank = lax.axis_index("tp")
    my_device = ctx_rank * tp_count + tp_rank
    segments = utterance_ids[0]
    encoded_rows = mel_frames.shape[0] // 8
    model_width = output_proj.shape[1]
    feature_part = model_width // tp_count
    slot_count = 3 * encoded_rows // (2 * ctx_count)
    ctx_steps = [("ctx", bit) for bit in range(axis_bits("ctx"))]
    tp_steps = [("tp", bit) for bit in range(axis_bits("tp"))]
    near, far = tp_steps[:1], tp_steps[1:]
    step_count = len(ctx_steps) + len(tp_steps)

    slot_index = jnp.arange(slot_count, dtype=jnp.int32)
    shard_id = jnp.arange(ctx_count, dtype=jnp.int32)
    pack_id = jnp.arange(device_count, dtype=jnp.int32)
    my_counts = lax.dynamic_index_in_dim(frame_counts, my_device, 0, keepdims=False)
    my_starts = jnp.sum(jnp.where(shard_id[None, :] < shard_id[:, None], my_counts[None, :], 0), 1)
    row_of_slot = jnp.where(
        slot_index[None, :] < my_counts[:, None], my_starts[:, None] + slot_index[None, :], -1
    ).reshape(-1)
    shard_counts = lax.dynamic_index_in_dim(frame_counts, ctx_rank, 1, keepdims=False)
    shard_starts = jnp.sum(
        jnp.where(pack_id[None, :] < pack_id[:, None], shard_counts[None, :], 0), 1
    )
    place_of_slot = jnp.where(
        slot_index[None, :] < shard_counts[:, None],
        shard_starts[:, None] + slot_index[None, :],
        -1,
    ).reshape(-1)
    local_rows = jnp.arange(encoded_rows, dtype=jnp.int32)
    places = [(tp_rank ^ flip) * encoded_rows + local_rows for flip in range(tp_count)]

    cot_blocks = gather_blocks(embed_grads, "tp")
    frame_back = jnp.concatenate(
        [
            lax.dot_general(
                cot, projector, (((1,), (1,)), ((), ())), preferred_element_type=jnp.float32
            ).astype(jnp.bfloat16)
            for cot in cot_blocks
        ]
    )
    parcel = pick(place_of_slot, jnp.concatenate(places), frame_back)
    returned = lax.all_to_all(
        parcel.reshape(device_count, slot_count, feature_part),
        ("ctx", "tp"),
        split_axis=0,
        concat_axis=0,
        tiled=True,
    )
    projector_blocks = gather_blocks(projector, "tp")

    inputs = subsample(mel_frames, input_proj, sub_depthwise, sub_pointwise, output_proj)
    encoded, kept_state = conv_forward(
        inputs, segments, norm_gain, pointwise_one, depthwise_taps, pointwise_two
    )
    normed, _, _, activated = kept_state
    outgoing = pick(row_of_slot, local_rows, encoded)
    outgoing = outgoing.reshape(ctx_count, slot_count, tp_count, feature_part)
    arrived = lax.all_to_all(
        outgoing.transpose(0, 2, 1, 3).reshape(device_count, slot_count, feature_part),
        ("ctx", "tp"),
        split_axis=0,
        concat_axis=0,
        tiled=True,
    ).reshape(device_count * slot_count, feature_part)

    returned = returned.reshape(ctx_count, tp_count, slot_count, feature_part)
    output_grad = pick(
        local_rows,
        row_of_slot,
        returned.transpose(0, 2, 1, 3).reshape(ctx_count * slot_count, model_width),
    )
    two_grad = rows_product(output_grad, activated).astype(jnp.bfloat16)
    two_part = fold_scatter(split_bits(two_grad, step_count), near + far + ctx_steps).T
    raised_grad = raised_backward(output_grad, segments, depthwise_taps, pointwise_two, kept_state)
    half = model_width // 2
    one_first = fold_scatter(
        split_bits(rows_product(raised_grad, normed[:, :half]).astype(jnp.bfloat16), step_count),
        near + far + ctx_steps,
    )
    one_second = fold_scatter(
        split_bits(rows_product(raised_grad, normed[:, half:]).astype(jnp.bfloat16), step_count),
        near + ctx_steps + far,
    )
    one_part = jnp.concatenate([one_first, one_second], axis=1).T

    frame_blocks = [pick(place, place_of_slot, arrived) for place in places]
    weight_sum = sum(rows_product(cot, held) for cot, held in zip(cot_blocks, frame_blocks))
    projector_grad = fold_scatter(
        split_bits(weight_sum.astype(jnp.bfloat16), len(ctx_steps)), ctx_steps
    ).T
    row_blocks = [frame_blocks[0]] + [
        exchange(frame_blocks[flip], "tp", flip) for flip in range(1, tp_count)
    ]
    llm_embed = sum(
        jnp.dot(held, weights, preferred_element_type=jnp.float32)
        for held, weights in zip(row_blocks, projector_blocks)
    ).astype(jnp.bfloat16)
    return (llm_embed, projector_grad, one_part, two_part)


def solution(mesh):
    placed = (
        P(("ctx", "tp"), None),
        P(("ctx", "tp"), None),
        P(),
        P(),
        P(),
        P(),
        P(),
        P(),
        P(),
        P(),
        P(),
        P("tp", None),
        P(("ctx", "tp"), None),
    )
    return jax.shard_map(
        body,
        mesh=mesh,
        in_specs=placed,
        out_specs=(
            P(("ctx", "tp"), None),
            P("tp", "ctx"),
            P(None, ("ctx", "tp")),
            P(None, ("ctx", "tp")),
        ),
        check_vma=False,
    )
```

```python
import jax
import jax.numpy as jnp
from jax import lax
from jax.sharding import PartitionSpec as P


def exchange(value, axis_name, flip):
    size = lax.axis_size(axis_name)
    return lax.ppermute(value, axis_name, [(rank, rank ^ flip) for rank in range(size)])


def axis_bits(axis_name):
    return lax.axis_size(axis_name).bit_length() - 1


def gather_blocks(block, axis_name):
    blocks = {0: block}
    for bit in reversed(range(axis_bits(axis_name))):
        for flip, held in list(blocks.items()):
            blocks[flip ^ (1 << bit)] = exchange(held, axis_name, 1 << bit)
    return [blocks[flip] for flip in range(lax.axis_size(axis_name))]


def fold_scatter(value, order, dims, last=False):
    layout = sorted(dims, key=lambda step: (step[0] != "ctx", -step[1]))
    for position, step in enumerate(order):
        axis_name, bit = step
        dim = layout.index(step)
        layout.remove(step)
        mine = (lax.axis_index(axis_name) >> bit) & 1
        keep = lax.dynamic_index_in_dim(value, mine, dim, keepdims=False)
        send = lax.dynamic_index_in_dim(value, 1 - mine, dim, keepdims=False)
        came = exchange(send, axis_name, 1 << bit)
        value = keep.astype(jnp.float32) + came.astype(jnp.float32)
        if not last or position + 1 < len(order):
            value = value.astype(jnp.bfloat16)
    return value


def split_bits(value, steps):
    return value.reshape((2,) * steps + (value.shape[0] >> steps,) + value.shape[1:])


def subsample(frames_in, input_proj, sub_depthwise, sub_pointwise, output_proj):
    encoded_rows = frames_in.shape[0] // 8
    channels = input_proj.shape[1]
    by_phase = frames_in.reshape(encoded_rows, 8, frames_in.shape[1]).transpose(1, 0, 2)
    hidden = jax.nn.relu(
        jnp.dot(
            by_phase.reshape(8 * encoded_rows, frames_in.shape[1]),
            input_proj,
            preferred_element_type=jnp.float32,
        )
    ).astype(jnp.bfloat16)
    length = 8
    for section_index in range(3):
        length = length // 2
        grouped = hidden.reshape(length, 2, encoded_rows, channels).astype(jnp.float32)
        tap_pair = sub_depthwise[section_index].astype(jnp.float32)
        strided = (grouped[:, 0] * tap_pair[0] + grouped[:, 1] * tap_pair[1]).astype(jnp.bfloat16)
        hidden = jax.nn.relu(
            jnp.dot(
                strided.reshape(length * encoded_rows, channels),
                sub_pointwise[section_index],
                preferred_element_type=jnp.float32,
            )
        ).astype(jnp.bfloat16)
    return jnp.dot(hidden, output_proj, preferred_element_type=jnp.float32)


def depthwise(values, segments, kernel):
    row_total = values.shape[0]
    padded = jnp.pad(values, ((4, 4), (0, 0)))
    padded_ids = jnp.pad(segments, 4, constant_values=-1)
    running_sum = jnp.zeros(values.shape, jnp.float32)
    for tap_index in range(9):
        same_utt = (padded_ids[tap_index : tap_index + row_total] == segments).astype(jnp.float32)[
            :, None
        ]
        running_sum = (
            running_sum + kernel[tap_index] * padded[tap_index : tap_index + row_total] * same_utt
        )
    return running_sum


def depthwise_back(grad_rows, segments, kernel):
    row_total = grad_rows.shape[0]
    padded_ids = jnp.pad(segments, 4, constant_values=-1)
    running_sum = jnp.zeros(grad_rows.shape, jnp.float32)
    for tap_index in range(9):
        same_utt = (padded_ids[tap_index : tap_index + row_total] == segments).astype(jnp.float32)[
            :, None
        ]
        moved_rows = jnp.pad(grad_rows * same_utt, ((4, 4), (0, 0)))
        running_sum = (
            running_sum + kernel[tap_index] * moved_rows[8 - tap_index : 8 - tap_index + row_total]
        )
    return running_sum


def conv_forward(inputs, segments, norm_gain, pointwise_one, depthwise_taps, pointwise_two):
    center = jnp.mean(inputs, axis=1, keepdims=True)
    spread = jnp.mean(jnp.square(inputs - center), axis=1, keepdims=True)
    normed = ((inputs - center) * lax.rsqrt(spread + 1e-05) * norm_gain.astype(jnp.float32)).astype(
        jnp.bfloat16
    )
    raised = jnp.dot(normed, pointwise_one, preferred_element_type=jnp.float32)
    model_width = inputs.shape[1]
    gated_rows = raised[:, :model_width] * jax.nn.sigmoid(raised[:, model_width:])
    mixed_rows = depthwise(gated_rows, segments, depthwise_taps.astype(jnp.float32))
    activated = (mixed_rows * jax.nn.sigmoid(mixed_rows)).astype(jnp.bfloat16)
    output = (
        inputs + jnp.dot(activated, pointwise_two, preferred_element_type=jnp.float32)
    ).astype(jnp.bfloat16)
    return (output, (normed, raised, mixed_rows, activated))


def raised_backward(output_grad, segments, depthwise_taps, pointwise_two, kept_state):
    _, raised, mixed_rows, _ = kept_state
    model_width = output_grad.shape[1]
    act_grad = lax.dot_general(
        output_grad,
        pointwise_two,
        (((1,), (1,)), ((), ())),
        preferred_element_type=jnp.float32,
    )
    sigmoid_mix = jax.nn.sigmoid(mixed_rows)
    mixed_grad = act_grad * (sigmoid_mix + mixed_rows * sigmoid_mix * (1.0 - sigmoid_mix))
    gated_grad = depthwise_back(mixed_grad, segments, depthwise_taps.astype(jnp.float32))
    sigmoid_gate = jax.nn.sigmoid(raised[:, model_width:])
    return jnp.concatenate(
        [
            gated_grad * sigmoid_gate,
            gated_grad * raised[:, :model_width] * sigmoid_gate * (1.0 - sigmoid_gate),
        ],
        axis=1,
    ).astype(jnp.bfloat16)


def rows_product(left, right):
    return lax.dot_general(
        left, right, (((0,), (0,)), ((), ())), preferred_element_type=jnp.float32
    )


def pick(wanted, slots, rows):
    chosen = (wanted[:, None] == slots[None, :]).astype(jnp.bfloat16)
    return jnp.dot(chosen, rows, preferred_element_type=jnp.float32).astype(jnp.bfloat16)


def body(
    mel_frames,
    utterance_ids,
    frame_counts,
    input_proj,
    sub_depthwise,
    sub_pointwise,
    output_proj,
    norm_gain,
    pointwise_one,
    depthwise_taps,
    pointwise_two,
    projector,
    embed_grads,
):
    ctx_count = lax.axis_size("ctx")
    tp_count = lax.axis_size("tp")
    device_count = ctx_count * tp_count
    ctx_rank = lax.axis_index("ctx")
    tp_rank = lax.axis_index("tp")
    my_device = ctx_rank * tp_count + tp_rank
    segments = utterance_ids[0]
    encoded_rows = mel_frames.shape[0] // 8
    model_width = output_proj.shape[1]
    feature_part = model_width // tp_count
    slot_count = 3 * encoded_rows // (2 * ctx_count)
    ctx_steps = [("ctx", bit) for bit in range(axis_bits("ctx"))]
    tp_steps = [("tp", bit) for bit in range(axis_bits("tp"))]
    near, far = tp_steps[:1], tp_steps[1:]
    step_count = len(ctx_steps) + len(tp_steps)

    slot_index = jnp.arange(slot_count, dtype=jnp.int32)
    shard_id = jnp.arange(ctx_count, dtype=jnp.int32)
    pack_id = jnp.arange(device_count, dtype=jnp.int32)
    my_counts = lax.dynamic_index_in_dim(frame_counts, my_device, 0, keepdims=False)
    my_starts = jnp.sum(jnp.where(shard_id[None, :] < shard_id[:, None], my_counts[None, :], 0), 1)
    row_of_slot = jnp.where(
        slot_index[None, :] < my_counts[:, None], my_starts[:, None] + slot_index[None, :], -1
    ).reshape(-1)
    shard_counts = lax.dynamic_index_in_dim(frame_counts, ctx_rank, 1, keepdims=False)
    shard_starts = jnp.sum(
        jnp.where(pack_id[None, :] < pack_id[:, None], shard_counts[None, :], 0), 1
    )
    place_of_slot = jnp.where(
        slot_index[None, :] < shard_counts[:, None],
        shard_starts[:, None] + slot_index[None, :],
        -1,
    )
    place_of_slot = (
        place_of_slot.reshape(ctx_count, tp_count, slot_count).transpose(1, 0, 2).reshape(-1)
    )
    local_rows = jnp.arange(encoded_rows, dtype=jnp.int32)
    places = [(tp_rank ^ flip) * encoded_rows + local_rows for flip in range(tp_count)]

    def spread(values):
        return lax.all_to_all(
            values.reshape(device_count, slot_count, feature_part),
            ("tp", "ctx"),
            split_axis=0,
            concat_axis=0,
            tiled=True,
        )

    cot_blocks = gather_blocks(embed_grads, "tp")
    frame_back = jnp.concatenate(
        [
            lax.dot_general(
                cot, projector, (((1,), (1,)), ((), ())), preferred_element_type=jnp.float32
            ).astype(jnp.bfloat16)
            for cot in cot_blocks
        ]
    )
    parcel = pick(place_of_slot, jnp.concatenate(places), frame_back)
    returned = spread(parcel)
    late_projector, _ = lax.optimization_barrier((projector, cot_blocks[-1]))
    projector_blocks = gather_blocks(late_projector, "tp")

    inputs = subsample(mel_frames, input_proj, sub_depthwise, sub_pointwise, output_proj)
    encoded, kept_state = conv_forward(
        inputs, segments, norm_gain, pointwise_one, depthwise_taps, pointwise_two
    )
    normed, _, _, activated = kept_state
    encoded, _ = lax.optimization_barrier((encoded, parcel))
    outgoing = jnp.concatenate(
        [pick(row_of_slot, local_rows, part) for part in jnp.split(encoded, tp_count, axis=1)]
    )
    returned, outgoing = lax.optimization_barrier((returned, outgoing))
    arrived = spread(outgoing).reshape(device_count * slot_count, feature_part)

    returned = returned.reshape(tp_count, ctx_count * slot_count, feature_part)
    output_grad = jnp.concatenate(
        [pick(local_rows, row_of_slot, returned[part]) for part in range(tp_count)], axis=1
    )
    two_grad = rows_product(output_grad, activated).astype(jnp.bfloat16)
    raised_grad = raised_backward(output_grad, segments, depthwise_taps, pointwise_two, kept_state)
    one_grad = rows_product(raised_grad, normed).astype(jnp.bfloat16)
    one_near = fold_scatter(split_bits(one_grad, step_count), near, ctx_steps + tp_steps)
    two_near = fold_scatter(split_bits(two_grad, step_count), near, ctx_steps + tp_steps)
    arrived, _ = lax.optimization_barrier((arrived, one_near))
    rest = ctx_steps + far
    half = one_near.shape[-2] // 2
    parts = [one_near[..., :half, :], one_near[..., half:, :], two_near]
    orders = [ctx_steps + far, ctx_steps[1:] + far + ctx_steps[:1], far + ctx_steps]
    parts = [fold_scatter(part, order[:1], rest) for part, order in zip(parts, orders)]
    after_first = parts[0], parts[1]
    parts = [
        fold_scatter(part, order[1:], [step for step in rest if step != order[0]], last=True)
        for part, order in zip(parts, orders)
    ]
    one_part = jnp.concatenate(parts[:2], axis=0).T
    two_part = parts[2].T

    frame_blocks = [pick(place, place_of_slot, arrived) for place in places]
    weight_sum = sum(rows_product(cot, held) for cot, held in zip(cot_blocks, frame_blocks))
    projector_grad = fold_scatter(
        split_bits(weight_sum.astype(jnp.bfloat16), len(ctx_steps)), ctx_steps, ctx_steps, last=True
    ).T
    row_blocks = [frame_blocks[0]] + [
        exchange(frame_blocks[flip], "tp", flip) for flip in range(1, tp_count)
    ]
    row_blocks, _ = lax.optimization_barrier((row_blocks, after_first))
    llm_embed = sum(
        jnp.dot(held, weights, preferred_element_type=jnp.float32)
        for held, weights in zip(row_blocks, projector_blocks)
    ).astype(jnp.bfloat16)
    return (llm_embed, projector_grad, one_part, two_part)


def solution(mesh):
    placed = (
        P(("ctx", "tp"), None),
        P(("ctx", "tp"), None),
        P(),
        P(),
        P(),
        P(),
        P(),
        P(),
        P(),
        P(),
        P(),
        P("tp", None),
        P(("ctx", "tp"), None),
    )
    return jax.shard_map(
        body,
        mesh=mesh,
        in_specs=placed,
        out_specs=(
            P(("ctx", "tp"), None),
            P("tp", "ctx"),
            P(None, ("ctx", "tp")),
            P(None, ("ctx", "tp")),
        ),
        check_vma=False,
    )
```

```python
import jax
import jax.numpy as jnp
from jax import lax
from jax.sharding import PartitionSpec as P


def exchange(value, axis_name, flip):
    size = lax.axis_size(axis_name)
    return lax.ppermute(value, axis_name, [(rank, rank ^ flip) for rank in range(size)])


def axis_bits(axis_name):
    return lax.axis_size(axis_name).bit_length() - 1


def gather_blocks(block, axis_name):
    blocks = {0: block}
    for bit in reversed(range(axis_bits(axis_name))):
        for flip, held in list(blocks.items()):
            blocks[flip ^ (1 << bit)] = exchange(held, axis_name, 1 << bit)
    return [blocks[flip] for flip in range(lax.axis_size(axis_name))]


def fold_step(value, dims, step, last=False):
    axis_name, bit = step
    dim = sorted(dims, key=lambda entry: (entry[0] != "ctx", -entry[1])).index(step)
    mine = (lax.axis_index(axis_name) >> bit) & 1
    keep = lax.dynamic_index_in_dim(value, mine, dim, keepdims=False)
    send = lax.dynamic_index_in_dim(value, 1 - mine, dim, keepdims=False)
    came = exchange(send, axis_name, 1 << bit)
    value = keep.astype(jnp.float32) + came.astype(jnp.float32)
    return value if last else value.astype(jnp.bfloat16)


def split_bits(value, steps):
    return value.reshape((2,) * steps + (value.shape[0] >> steps,) + value.shape[1:])


def subsample(frames_in, input_proj, sub_depthwise, sub_pointwise, output_proj):
    encoded_rows = frames_in.shape[0] // 8
    channels = input_proj.shape[1]
    by_phase = frames_in.reshape(encoded_rows, 8, frames_in.shape[1]).transpose(1, 0, 2)
    hidden = jax.nn.relu(
        jnp.dot(
            by_phase.reshape(8 * encoded_rows, frames_in.shape[1]),
            input_proj,
            preferred_element_type=jnp.float32,
        )
    ).astype(jnp.bfloat16)
    length = 8
    for section_index in range(3):
        length = length // 2
        grouped = hidden.reshape(length, 2, encoded_rows, channels).astype(jnp.float32)
        tap_pair = sub_depthwise[section_index].astype(jnp.float32)
        strided = (grouped[:, 0] * tap_pair[0] + grouped[:, 1] * tap_pair[1]).astype(jnp.bfloat16)
        hidden = jax.nn.relu(
            jnp.dot(
                strided.reshape(length * encoded_rows, channels),
                sub_pointwise[section_index],
                preferred_element_type=jnp.float32,
            )
        ).astype(jnp.bfloat16)
    return jnp.dot(hidden, output_proj, preferred_element_type=jnp.float32)


def depthwise(values, segments, kernel):
    row_total = values.shape[0]
    padded = jnp.pad(values, ((4, 4), (0, 0)))
    padded_ids = jnp.pad(segments, 4, constant_values=-1)
    running_sum = jnp.zeros(values.shape, jnp.float32)
    for tap_index in range(9):
        same_utt = (padded_ids[tap_index : tap_index + row_total] == segments).astype(jnp.float32)[
            :, None
        ]
        running_sum = (
            running_sum + kernel[tap_index] * padded[tap_index : tap_index + row_total] * same_utt
        )
    return running_sum


def depthwise_back(grad_rows, segments, kernel):
    row_total = grad_rows.shape[0]
    padded_ids = jnp.pad(segments, 4, constant_values=-1)
    running_sum = jnp.zeros(grad_rows.shape, jnp.float32)
    for tap_index in range(9):
        same_utt = (padded_ids[tap_index : tap_index + row_total] == segments).astype(jnp.float32)[
            :, None
        ]
        moved_rows = jnp.pad(grad_rows * same_utt, ((4, 4), (0, 0)))
        running_sum = (
            running_sum + kernel[tap_index] * moved_rows[8 - tap_index : 8 - tap_index + row_total]
        )
    return running_sum


def conv_forward(inputs, segments, norm_gain, pointwise_one, depthwise_taps, pointwise_two):
    center = jnp.mean(inputs, axis=1, keepdims=True)
    spread = jnp.mean(jnp.square(inputs - center), axis=1, keepdims=True)
    normed = ((inputs - center) * lax.rsqrt(spread + 1e-05) * norm_gain.astype(jnp.float32)).astype(
        jnp.bfloat16
    )
    raised = jnp.dot(normed, pointwise_one, preferred_element_type=jnp.float32)
    model_width = inputs.shape[1]
    gated_rows = raised[:, :model_width] * jax.nn.sigmoid(raised[:, model_width:])
    mixed_rows = depthwise(gated_rows, segments, depthwise_taps.astype(jnp.float32))
    activated = (mixed_rows * jax.nn.sigmoid(mixed_rows)).astype(jnp.bfloat16)
    output = (
        inputs + jnp.dot(activated, pointwise_two, preferred_element_type=jnp.float32)
    ).astype(jnp.bfloat16)
    return (output, (normed, raised, mixed_rows, activated))


def raised_backward(output_grad, segments, depthwise_taps, pointwise_two, kept_state):
    _, raised, mixed_rows, _ = kept_state
    model_width = output_grad.shape[1]
    act_grad = lax.dot_general(
        output_grad, pointwise_two, (((1,), (1,)), ((), ())), preferred_element_type=jnp.float32
    )
    sigmoid_mix = jax.nn.sigmoid(mixed_rows)
    mixed_grad = act_grad * (sigmoid_mix + mixed_rows * sigmoid_mix * (1.0 - sigmoid_mix))
    gated_grad = depthwise_back(mixed_grad, segments, depthwise_taps.astype(jnp.float32))
    sigmoid_gate = jax.nn.sigmoid(raised[:, model_width:])
    return jnp.concatenate(
        [
            gated_grad * sigmoid_gate,
            gated_grad * raised[:, :model_width] * sigmoid_gate * (1.0 - sigmoid_gate),
        ],
        axis=1,
    ).astype(jnp.bfloat16)


def rows_product(left, right):
    return lax.dot_general(
        left, right, (((0,), (0,)), ((), ())), preferred_element_type=jnp.float32
    )


def pick(wanted, slots, rows):
    chosen = (wanted[:, None] == slots[None, :]).astype(jnp.bfloat16)
    return jnp.dot(chosen, rows, preferred_element_type=jnp.float32).astype(jnp.bfloat16)


def body(
    mel_frames,
    utterance_ids,
    frame_counts,
    input_proj,
    sub_depthwise,
    sub_pointwise,
    output_proj,
    norm_gain,
    pointwise_one,
    depthwise_taps,
    pointwise_two,
    projector,
    embed_grads,
):
    ctx_count = lax.axis_size("ctx")
    tp_count = lax.axis_size("tp")
    device_count = ctx_count * tp_count
    ctx_rank = lax.axis_index("ctx")
    tp_rank = lax.axis_index("tp")
    my_device = ctx_rank * tp_count + tp_rank
    segments = utterance_ids[0]
    encoded_rows = mel_frames.shape[0] // 8
    model_width = output_proj.shape[1]
    feature_part = model_width // tp_count
    slot_count = 3 * encoded_rows // (2 * ctx_count)
    ctx_steps = [("ctx", bit) for bit in range(axis_bits("ctx"))]
    tp_steps = [("tp", bit) for bit in range(axis_bits("tp"))]
    far = tp_steps[1:]
    step_count = len(ctx_steps) + len(tp_steps)

    slot_index = jnp.arange(slot_count, dtype=jnp.int32)
    shard_id = jnp.arange(ctx_count, dtype=jnp.int32)
    pack_id = jnp.arange(device_count, dtype=jnp.int32)
    my_counts = lax.dynamic_index_in_dim(frame_counts, my_device, 0, keepdims=False)
    my_starts = jnp.sum(jnp.where(shard_id[None, :] < shard_id[:, None], my_counts[None, :], 0), 1)
    row_of_slot = jnp.where(
        slot_index[None, :] < my_counts[:, None], my_starts[:, None] + slot_index[None, :], -1
    ).reshape(-1)
    shard_counts = lax.dynamic_index_in_dim(frame_counts, ctx_rank, 1, keepdims=False)
    shard_starts = jnp.sum(
        jnp.where(pack_id[None, :] < pack_id[:, None], shard_counts[None, :], 0), 1
    )
    place_of_slot = jnp.where(
        slot_index[None, :] < shard_counts[:, None],
        shard_starts[:, None] + slot_index[None, :],
        -1,
    )
    place_of_slot = (
        place_of_slot.reshape(ctx_count, tp_count, slot_count).transpose(1, 0, 2).reshape(-1)
    )
    local_rows = jnp.arange(encoded_rows, dtype=jnp.int32)
    places = [(tp_rank ^ flip) * encoded_rows + local_rows for flip in range(tp_count)]

    def spread(values):
        return lax.all_to_all(
            values.reshape(device_count, slot_count, feature_part),
            ("tp", "ctx"),
            split_axis=0,
            concat_axis=0,
            tiled=True,
        )

    cot_blocks = gather_blocks(embed_grads, "tp")
    frame_back = jnp.concatenate(
        [
            lax.dot_general(
                cot, projector, (((1,), (1,)), ((), ())), preferred_element_type=jnp.float32
            ).astype(jnp.bfloat16)
            for cot in cot_blocks
        ]
    )
    placing = lax.optimization_barrier(
        (jnp.concatenate(places)[:, None] == place_of_slot[None, :]).astype(jnp.bfloat16)
    )
    parcel = rows_product(placing, frame_back).astype(jnp.bfloat16)
    returned = spread(parcel)
    late_projector, _ = lax.optimization_barrier((projector, cot_blocks[tp_count // 2]))
    projector_blocks = gather_blocks(late_projector, "tp")

    inputs = subsample(mel_frames, input_proj, sub_depthwise, sub_pointwise, output_proj)
    encoded, kept_state = conv_forward(
        inputs, segments, norm_gain, pointwise_one, depthwise_taps, pointwise_two
    )
    normed, _, _, activated = kept_state
    encoded, _ = lax.optimization_barrier((encoded, parcel))
    outgoing = jnp.concatenate(
        [pick(row_of_slot, local_rows, part) for part in jnp.split(encoded, tp_count, axis=1)]
    )
    returned, outgoing, projector_blocks = lax.optimization_barrier(
        (returned, outgoing, projector_blocks)
    )
    arrived = spread(outgoing).reshape(device_count * slot_count, feature_part)

    returned = returned.reshape(tp_count, ctx_count * slot_count, feature_part)
    output_grad = jnp.concatenate(
        [pick(local_rows, row_of_slot, returned[part]) for part in range(tp_count)], axis=1
    )
    two_grad = rows_product(output_grad, activated).astype(jnp.bfloat16)
    raised_grad = raised_backward(output_grad, segments, depthwise_taps, pointwise_two, kept_state)
    one_grad = rows_product(raised_grad, normed).astype(jnp.bfloat16)
    all_steps = ctx_steps + tp_steps
    near = tp_steps[0]
    two_near = fold_step(split_bits(two_grad, step_count), all_steps, near)
    one_near = fold_step(split_bits(one_grad, step_count), all_steps, near)
    one_near, two_near = lax.optimization_barrier((one_near, two_near))
    arrived, _ = lax.optimization_barrier((arrived, one_near))
    half = one_near.shape[-2] // 2
    parts = [one_near[..., :half, :], one_near[..., half:, :], two_near]
    orders = [ctx_steps + far, ctx_steps[1:] + far + ctx_steps[:1], far + ctx_steps]

    def advance(parts, position):
        return [
            fold_step(part, order[position:], order[position], position + 1 == len(order))
            for part, order in zip(parts, orders)
        ]

    parts = advance(parts, 0)
    framed = jnp.dot(placing, arrived, preferred_element_type=jnp.float32)
    framed = framed.astype(jnp.bfloat16)
    parts = lax.optimization_barrier(parts)
    frame_blocks = jnp.split(framed, tp_count)
    row_blocks = [frame_blocks[0]] + [
        exchange(frame_blocks[flip], "tp", flip) for flip in range(1, tp_count)
    ]
    weight_sum = sum(rows_product(cot, held) for cot, held in zip(cot_blocks, frame_blocks))
    weight = split_bits(weight_sum.astype(jnp.bfloat16), len(ctx_steps))
    row_blocks, _ = lax.optimization_barrier((row_blocks, parts))
    llm_embed = sum(
        jnp.dot(held, weights, preferred_element_type=jnp.float32)
        for held, weights in zip(row_blocks, projector_blocks)
    ).astype(jnp.bfloat16)
    left = len(orders[0]) - len(ctx_steps) + 1
    for position in range(1, left):
        parts = lax.optimization_barrier(advance(parts, position))
    for taken, position in enumerate(range(left, len(orders[0]))):
        weight = fold_step(weight, ctx_steps[taken:], ctx_steps[taken])
        parts, weight = lax.optimization_barrier((advance(parts, position), weight))
    projector_grad = fold_step(weight, ctx_steps[-1:], ctx_steps[-1], last=True).T
    one_part = jnp.concatenate(parts[:2], axis=0).T
    two_part = parts[2].T
    return (llm_embed, projector_grad, one_part, two_part)


def solution(mesh):
    placed = (
        P(("ctx", "tp"), None),
        P(("ctx", "tp"), None),
        P(),
        P(),
        P(),
        P(),
        P(),
        P(),
        P(),
        P(),
        P(),
        P("tp", None),
        P(("ctx", "tp"), None),
    )
    return jax.shard_map(
        body,
        mesh=mesh,
        in_specs=placed,
        out_specs=(
            P(("ctx", "tp"), None),
            P("tp", "ctx"),
            P(None, ("ctx", "tp")),
            P(None, ("ctx", "tp")),
        ),
        check_vma=False,
    )
```

```python
import jax
import jax.numpy as jnp
from jax import lax
from jax.sharding import PartitionSpec as P


def exchange(value, axis_name, flip):
    size = lax.axis_size(axis_name)
    return lax.ppermute(value, axis_name, [(rank, rank ^ flip) for rank in range(size)])


def axis_bits(axis_name):
    return lax.axis_size(axis_name).bit_length() - 1


def gather_blocks(block, axis_name):
    blocks = {0: block}
    for bit in reversed(range(axis_bits(axis_name))):
        for flip, held in list(blocks.items()):
            blocks[flip ^ (1 << bit)] = exchange(held, axis_name, 1 << bit)
    return [blocks[flip] for flip in range(lax.axis_size(axis_name))]


def fold_step(value, dims, step, last=False):
    axis_name, bit = step
    dim = sorted(dims, key=lambda entry: (entry[0] != "ctx", -entry[1])).index(step)
    mine = (lax.axis_index(axis_name) >> bit) & 1
    keep = lax.dynamic_index_in_dim(value, mine, dim, keepdims=False)
    send = lax.dynamic_index_in_dim(value, 1 - mine, dim, keepdims=False)
    came = exchange(send, axis_name, 1 << bit)
    value = keep.astype(jnp.float32) + came.astype(jnp.float32)
    return value if last else value.astype(jnp.bfloat16)


def fold_last(value, dims):
    dims = sorted(dims, key=lambda entry: (entry[0] != "ctx", -entry[1]))
    tp_bits = axis_bits("tp")
    devices = lax.axis_size("ctx") * lax.axis_size("tp")
    mine = [(lax.axis_index(axis_name) >> bit) & 1 for axis_name, bit in dims]
    weights = [1 << (bit + (tp_bits if axis_name == "ctx" else 0)) for axis_name, bit in dims]
    total = None
    for first in range(2):
        for second in range(2):
            block = lax.dynamic_index_in_dim(value, mine[0] ^ first, 0, keepdims=False)
            block = lax.dynamic_index_in_dim(block, mine[1] ^ second, 0, keepdims=False)
            flip = first * weights[0] + second * weights[1]
            if flip:
                block = lax.ppermute(
                    block, ("ctx", "tp"), [(rank, rank ^ flip) for rank in range(devices)]
                )
            block = block.astype(jnp.float32)
            total = block if total is None else total + block
    return total


def split_bits(value, steps):
    return value.reshape((2,) * steps + (value.shape[0] >> steps,) + value.shape[1:])


def subsample(frames_in, input_proj, sub_depthwise, sub_pointwise, output_proj):
    encoded_rows = frames_in.shape[0] // 8
    channels = input_proj.shape[1]
    by_phase = frames_in.reshape(encoded_rows, 8, frames_in.shape[1]).transpose(1, 0, 2)
    hidden = jax.nn.relu(
        jnp.dot(
            by_phase.reshape(8 * encoded_rows, frames_in.shape[1]),
            input_proj,
            preferred_element_type=jnp.float32,
        )
    ).astype(jnp.bfloat16)
    length = 8
    for section_index in range(3):
        length = length // 2
        grouped = hidden.reshape(length, 2, encoded_rows, channels).astype(jnp.float32)
        tap_pair = sub_depthwise[section_index].astype(jnp.float32)
        strided = (grouped[:, 0] * tap_pair[0] + grouped[:, 1] * tap_pair[1]).astype(jnp.bfloat16)
        hidden = jax.nn.relu(
            jnp.dot(
                strided.reshape(length * encoded_rows, channels),
                sub_pointwise[section_index],
                preferred_element_type=jnp.float32,
            )
        ).astype(jnp.bfloat16)
    return jnp.dot(hidden, output_proj, preferred_element_type=jnp.float32)


def depthwise(values, segments, kernel):
    row_total = values.shape[0]
    padded = jnp.pad(values, ((4, 4), (0, 0)))
    padded_ids = jnp.pad(segments, 4, constant_values=-1)
    running_sum = jnp.zeros(values.shape, jnp.float32)
    for tap_index in range(9):
        same_utt = (padded_ids[tap_index : tap_index + row_total] == segments).astype(jnp.float32)[
            :, None
        ]
        running_sum = (
            running_sum + kernel[tap_index] * padded[tap_index : tap_index + row_total] * same_utt
        )
    return running_sum


def depthwise_back(grad_rows, segments, kernel):
    row_total = grad_rows.shape[0]
    padded_ids = jnp.pad(segments, 4, constant_values=-1)
    running_sum = jnp.zeros(grad_rows.shape, jnp.float32)
    for tap_index in range(9):
        same_utt = (padded_ids[tap_index : tap_index + row_total] == segments).astype(jnp.float32)[
            :, None
        ]
        moved_rows = jnp.pad(grad_rows * same_utt, ((4, 4), (0, 0)))
        running_sum = (
            running_sum + kernel[tap_index] * moved_rows[8 - tap_index : 8 - tap_index + row_total]
        )
    return running_sum


def conv_forward(inputs, segments, norm_gain, pointwise_one, depthwise_taps, pointwise_two):
    center = jnp.mean(inputs, axis=1, keepdims=True)
    spread = jnp.mean(jnp.square(inputs - center), axis=1, keepdims=True)
    normed = ((inputs - center) * lax.rsqrt(spread + 1e-05) * norm_gain.astype(jnp.float32)).astype(
        jnp.bfloat16
    )
    raised = jnp.dot(normed, pointwise_one, preferred_element_type=jnp.float32)
    model_width = inputs.shape[1]
    gated_rows = raised[:, :model_width] * jax.nn.sigmoid(raised[:, model_width:])
    mixed_rows = depthwise(gated_rows, segments, depthwise_taps.astype(jnp.float32))
    activated = (mixed_rows * jax.nn.sigmoid(mixed_rows)).astype(jnp.bfloat16)
    output = (
        inputs + jnp.dot(activated, pointwise_two, preferred_element_type=jnp.float32)
    ).astype(jnp.bfloat16)
    return (output, (normed, raised, mixed_rows, activated))


def raised_backward(output_grad, segments, depthwise_taps, pointwise_two, kept_state):
    _, raised, mixed_rows, _ = kept_state
    model_width = output_grad.shape[1]
    act_grad = lax.dot_general(
        output_grad, pointwise_two, (((1,), (1,)), ((), ())), preferred_element_type=jnp.float32
    )
    sigmoid_mix = jax.nn.sigmoid(mixed_rows)
    mixed_grad = act_grad * (sigmoid_mix + mixed_rows * sigmoid_mix * (1.0 - sigmoid_mix))
    gated_grad = depthwise_back(mixed_grad, segments, depthwise_taps.astype(jnp.float32))
    sigmoid_gate = jax.nn.sigmoid(raised[:, model_width:])
    return jnp.concatenate(
        [
            gated_grad * sigmoid_gate,
            gated_grad * raised[:, :model_width] * sigmoid_gate * (1.0 - sigmoid_gate),
        ],
        axis=1,
    ).astype(jnp.bfloat16)


def rows_product(left, right):
    return lax.dot_general(
        left, right, (((0,), (0,)), ((), ())), preferred_element_type=jnp.float32
    )


def pick(wanted, slots, rows):
    chosen = (wanted[:, None] == slots[None, :]).astype(jnp.bfloat16)
    return jnp.dot(chosen, rows, preferred_element_type=jnp.float32).astype(jnp.bfloat16)


def body(
    mel_frames,
    utterance_ids,
    frame_counts,
    input_proj,
    sub_depthwise,
    sub_pointwise,
    output_proj,
    norm_gain,
    pointwise_one,
    depthwise_taps,
    pointwise_two,
    projector,
    embed_grads,
):
    ctx_count = lax.axis_size("ctx")
    tp_count = lax.axis_size("tp")
    device_count = ctx_count * tp_count
    ctx_rank = lax.axis_index("ctx")
    tp_rank = lax.axis_index("tp")
    my_device = ctx_rank * tp_count + tp_rank
    segments = utterance_ids[0]
    encoded_rows = mel_frames.shape[0] // 8
    model_width = output_proj.shape[1]
    feature_part = model_width // tp_count
    slot_count = 3 * encoded_rows // (2 * ctx_count)
    ctx_steps = [("ctx", bit) for bit in range(axis_bits("ctx"))]
    tp_steps = [("tp", bit) for bit in range(axis_bits("tp"))]
    far = tp_steps[1:]
    step_count = len(ctx_steps) + len(tp_steps)

    slot_index = jnp.arange(slot_count, dtype=jnp.int32)
    shard_id = jnp.arange(ctx_count, dtype=jnp.int32)
    pack_id = jnp.arange(device_count, dtype=jnp.int32)
    my_counts = lax.dynamic_index_in_dim(frame_counts, my_device, 0, keepdims=False)
    my_starts = jnp.sum(jnp.where(shard_id[None, :] < shard_id[:, None], my_counts[None, :], 0), 1)
    row_of_slot = jnp.where(
        slot_index[None, :] < my_counts[:, None], my_starts[:, None] + slot_index[None, :], -1
    ).reshape(-1)
    shard_counts = lax.dynamic_index_in_dim(frame_counts, ctx_rank, 1, keepdims=False)
    shard_starts = jnp.sum(
        jnp.where(pack_id[None, :] < pack_id[:, None], shard_counts[None, :], 0), 1
    )
    place_of_slot = jnp.where(
        slot_index[None, :] < shard_counts[:, None],
        shard_starts[:, None] + slot_index[None, :],
        -1,
    )
    place_of_slot = (
        place_of_slot.reshape(ctx_count, tp_count, slot_count).transpose(1, 0, 2).reshape(-1)
    )
    local_rows = jnp.arange(encoded_rows, dtype=jnp.int32)
    places = [(tp_rank ^ flip) * encoded_rows + local_rows for flip in range(tp_count)]

    def spread(values):
        return lax.all_to_all(
            values.reshape(device_count, slot_count, feature_part),
            ("tp", "ctx"),
            split_axis=0,
            concat_axis=0,
            tiled=True,
        )

    cot_blocks = gather_blocks(embed_grads, "tp")
    frame_back = jnp.concatenate(
        [
            lax.dot_general(
                cot, projector, (((1,), (1,)), ((), ())), preferred_element_type=jnp.float32
            ).astype(jnp.bfloat16)
            for cot in cot_blocks
        ]
    )
    placing = lax.optimization_barrier(
        (jnp.concatenate(places)[:, None] == place_of_slot[None, :]).astype(jnp.bfloat16)
    )
    parcel = rows_product(placing, frame_back).astype(jnp.bfloat16)
    returned = spread(parcel)
    late_projector, _ = lax.optimization_barrier((projector, cot_blocks[tp_count // 2]))
    projector_blocks = gather_blocks(late_projector, "tp")

    inputs = subsample(mel_frames, input_proj, sub_depthwise, sub_pointwise, output_proj)
    encoded, kept_state = conv_forward(
        inputs, segments, norm_gain, pointwise_one, depthwise_taps, pointwise_two
    )
    normed, _, _, activated = kept_state
    encoded, _ = lax.optimization_barrier((encoded, parcel))
    outgoing = jnp.concatenate(
        [pick(row_of_slot, local_rows, part) for part in jnp.split(encoded, tp_count, axis=1)]
    )
    returned, outgoing, projector_blocks = lax.optimization_barrier(
        (returned, outgoing, projector_blocks)
    )
    arrived = spread(outgoing).reshape(device_count * slot_count, feature_part)

    returned = returned.reshape(tp_count, ctx_count * slot_count, feature_part)
    output_grad = jnp.concatenate(
        [pick(local_rows, row_of_slot, returned[part]) for part in range(tp_count)], axis=1
    )
    two_grad = rows_product(output_grad, activated).astype(jnp.bfloat16)
    output_grad, two_grad = lax.optimization_barrier((output_grad, two_grad))
    raised_grad = raised_backward(output_grad, segments, depthwise_taps, pointwise_two, kept_state)
    one_grad = rows_product(raised_grad, normed).astype(jnp.bfloat16)
    all_steps = ctx_steps + tp_steps
    near = tp_steps[0]
    two_near = fold_step(split_bits(two_grad, step_count), all_steps, near)
    one_near = fold_step(split_bits(one_grad, step_count), all_steps, near)
    one_near, two_near = lax.optimization_barrier((one_near, two_near))
    arrived, _ = lax.optimization_barrier((arrived, one_near))
    half = one_near.shape[-2] // 2
    parts = [one_near[..., :half, :], one_near[..., half:, :], two_near]
    orders = [ctx_steps + far, ctx_steps[1:] + far + ctx_steps[:1], far + ctx_steps]

    def advance(parts, position):
        return [
            fold_step(part, order[position:], order[position], position + 1 == len(order))
            for part, order in zip(parts, orders)
        ]

    parts = advance(parts, 0)
    framed = jnp.dot(placing, arrived, preferred_element_type=jnp.float32)
    framed = framed.astype(jnp.bfloat16)
    parts = lax.optimization_barrier(parts)
    frame_blocks = jnp.split(framed, tp_count)
    row_blocks = [frame_blocks[0]] + [
        exchange(frame_blocks[flip], "tp", flip) for flip in range(1, tp_count)
    ]
    weight_sum = sum(rows_product(cot, held) for cot, held in zip(cot_blocks, frame_blocks))
    weight = split_bits(weight_sum.astype(jnp.bfloat16), len(ctx_steps))
    row_blocks, _ = lax.optimization_barrier((row_blocks, parts))
    llm_embed = sum(
        jnp.dot(held, weights, preferred_element_type=jnp.float32)
        for held, weights in zip(row_blocks, projector_blocks)
    ).astype(jnp.bfloat16)
    count = len(orders[0])
    for position in range(1, count - 2):
        taken = position - (count - len(ctx_steps))
        if taken >= 0:
            weight = fold_step(weight, ctx_steps[taken:], ctx_steps[taken])
        parts, weight = lax.optimization_barrier((advance(parts, position), weight))
    parts = [fold_last(part, order[-2:]) for part, order in zip(parts, orders)]
    projector_grad = fold_last(weight, ctx_steps[-2:]).T
    one_part = jnp.concatenate(parts[:2], axis=0).T
    two_part = parts[2].T
    return (llm_embed, projector_grad, one_part, two_part)


def solution(mesh):
    placed = (
        P(("ctx", "tp"), None),
        P(("ctx", "tp"), None),
        P(),
        P(),
        P(),
        P(),
        P(),
        P(),
        P(),
        P(),
        P(),
        P("tp", None),
        P(("ctx", "tp"), None),
    )
    return jax.shard_map(
        body,
        mesh=mesh,
        in_specs=placed,
        out_specs=(
            P(("ctx", "tp"), None),
            P("tp", "ctx"),
            P(None, ("ctx", "tp")),
            P(None, ("ctx", "tp")),
        ),
        check_vma=False,
    )
```
